32 devices in a mesh: replica: 8 (over z, core), shard: 4 (over y, x).
Axes of the slice: x: 2, y: 2, z: 4, core: 2. Of those that a mesh axis runs over, the one named last changes fastest.
Arguments:
- tokens: bfloat16 [32768, 2560], P(('replica', 'shard')), may hold values from -6 to 6
- w_in: bfloat16 [2560, 10496], P('shard'), may hold values from -0.125 to 0.125
- w_dt: bfloat16 [2560, 80], P('shard'), may hold values from -0.125 to 0.125
- w_out: bfloat16 [5120, 2560], P('shard'), may hold values from -0.078125 to 0.078125
- norm_gain: float32 [2560], replicated, may hold values from 0.5 to 1.5
- conv_weight: float32 [4, 5376], replicated, may hold values from -3 to 3
- conv_bias: float32 [5376], replicated, may hold values from -1.5 to 1.5
- dt_bias: float32 [80], replicated, may hold values from -5 to -1
- a_log: float32 [80], replicated, may hold values from -3 to 2.5
- d_skip: float32 [80], replicated, may hold values from 0.5 to 1.5
- gate_gain: float32 [5120], replicated, may hold values from 0.5 to 1.5
- cotangent: bfloat16 [32768, 2560], P(('replica', 'shard')), may hold values from -8 to 8
Outputs:
- result: bfloat16 [32768, 2560], P(('replica', 'shard'))
- token_grad: float32 [32768, 2560], P(('replica', 'shard'))
- grad_w_in: float32 [2560, 10496], P('shard')
- grad_w_dt: float32 [2560, 80], P('shard')
- grad_w_out: float32 [5120, 2560], P('shard')
- grad_norm_gain: float32 [2560], replicated
- grad_conv_weight: float32 [4, 5376], replicated
- grad_conv_bias: float32 [5376], replicated
- grad_dt_bias: float32 [80], replicated
- grad_a_log: float32 [80], replicated
- grad_d_skip: float32 [80], replicated
- grad_gate_gain: float32 [5120], replicated
The draws below stay inside these ranges and needn't reach their ends.
All inputs are finite; a program needn't handle non-finite values.
Results may differ from the reference program's by a relative error of at most 0.017.
Values may be sent and summed in bfloat16 or wider, within the bound.
No kernel may reach another device: no remote copies, remote signals or barrier semaphores. Data moves between devices by JAX's collectives and lax.ppermute only.
A program may use at most 768 MiB of HBM per device.

```python
import jax
import jax.numpy as jnp
from jax import lax

D = 2560
H = 80
P_SIZE = 64
E = 5120
NST = 128
CONVK = 4
SPAN = 256
SEQ = 1024
CH = 5376
ZX = 10496
TOKENS = 32768


def draw_cotangent(key, part):
    positions = jnp.arange(TOKENS, dtype=jnp.float32)
    scaling = 0.5 + 1.5 * positions / TOKENS
    noise = jnp.clip(jax.random.normal(key, (TOKENS, D), jnp.float32), -4.0, 4.0)
    return (noise * scaling[:, None]).astype(jnp.bfloat16)


def levels(own_key, extent, shards, low, top_value):
    factor_of = 1.0
    for axis_at, blocks in shards:
        steps = jax.random.uniform(jax.random.fold_in(jax.random.fold_in(own_key, 6), axis_at), (blocks,), jnp.float32, low / len(shards), top_value / len(shards))
        factor_of = factor_of * jnp.repeat(jnp.exp(steps), extent[axis_at] // blocks).reshape((-1,) + (1,) * (len(extent) - 1 - axis_at))
    return factor_of


def normal_values(rng, shape, spread, limit, shards=(), kind=jnp.bfloat16):
    values = jax.random.normal(rng, shape, jnp.float32) * spread
    if len(shards) > 0:
        values = levels(rng, shape, shards, -0.22, 0.18) * values
    return jnp.clip(values, min=-limit, max=limit).astype(kind)


def setup_inputs(seed: int = 0) -> dict:
    arg_keys = jax.random.split(jax.random.key(seed), 13)
    tokens = normal_values(arg_keys[0], (TOKENS, D), 1.0, 6.0, ((0, 32),))
    w_in = normal_values(arg_keys[1], (D, ZX), D ** -0.5, 0.125, ((0, 4),))
    w_dt = normal_values(arg_keys[2], (D, H), D ** -0.5, 0.125, ((0, 4),))
    w_out = normal_values(arg_keys[3], (E, D), E ** -0.5, 0.078125, ((0, 4),))
    norm_gain = jnp.clip(1.0 + 0.1 * jax.random.normal(arg_keys[4], (D,), jnp.float32), 0.5, 1.5)
    conv_weight = normal_values(arg_keys[5], (CONVK, CH), CONVK ** -0.5, 3.0, (), jnp.float32)
    conv_bias = normal_values(arg_keys[6], (CH,), 0.3, 1.5, (), jnp.float32)
    dt_bias = jnp.clip(jax.random.uniform(arg_keys[7], (H,), jnp.float32, -5.0, -1.0), -5.0, -1.0)
    a_log = jnp.clip(jax.random.uniform(arg_keys[8], (H,), jnp.float32, -3.0, 2.5), -3.0, 2.5)
    d_skip = jnp.clip(jax.random.uniform(arg_keys[9], (H,), jnp.float32, 0.5, 1.5), 0.5, 1.5)
    gate_gain = jnp.clip(1.0 + 0.1 * jax.random.normal(arg_keys[10], (E,), jnp.float32), 0.5, 1.5)
    cotangent = draw_cotangent(jax.random.fold_in(arg_keys[12], 71), 0)
    return {"tokens": tokens, "w_in": w_in, "w_dt": w_dt, "w_out": w_out, "norm_gain": norm_gain, "conv_weight": conv_weight, "conv_bias": conv_bias, "dt_bias": dt_bias, "a_log": a_log, "d_skip": d_skip, "gate_gain": gate_gain, "cotangent": cotangent}


eps = 1e-05

def rms_norm(tokens_f, gain):
    return tokens_f * lax.rsqrt(lax.optimization_barrier(jnp.mean(tokens_f * tokens_f, axis=-1, keepdims=True)) + eps) * gain

def contract_rows(left, right):
    return lax.dot_general(left, right, (((0,), (0,)), ((), ())), preferred_element_type=jnp.float32)

def contract_cols(left, right):
    return lax.dot_general(left, right, (((1,), (1,)), ((), ())), preferred_element_type=jnp.float32)

def ssd_scan(values, step_size, log_decay, in_state, out_state):
    length = values.shape[0]
    blocks = length // SPAN
    highest = lax.Precision.HIGHEST
    values4 = values.reshape(blocks, SPAN, H, P_SIZE)
    decay_blk = log_decay.reshape(blocks, SPAN, H).transpose(0, 2, 1)
    step_blk = step_size.reshape(blocks, SPAN, H).transpose(0, 2, 1)
    in_blk = in_state.reshape(blocks, SPAN, NST)
    out_blk = out_state.reshape(blocks, SPAN, NST)
    running = jnp.cumsum(decay_blk, axis=2)
    gap = running[:, :, :, None] - running[:, :, None, :]
    lower = jnp.tril(jnp.ones((SPAN, SPAN), dtype=bool))
    weights = jnp.where(lower, jnp.exp(jnp.where(lower, gap, 0.0)), 0.0)
    intersection = jnp.einsum('bln,bsn->bls', out_blk, in_blk, precision=highest)
    scores = weights * intersection[:, None, :, :] * step_blk[:, :, None, :]
    inner = jnp.einsum('bhls,bshp->blhp', scores, values4, precision=highest)
    to_end = jnp.exp(running[:, :, -1:] - running) * step_blk
    local = jnp.einsum('bsn,bhs,bshp->bhpn', in_blk, to_end, values4, precision=highest)
    whole_decay = jnp.exp(running[:, :, -1])

    def carry_state(state, item):
        decay_now, add_now = item
        return (state * decay_now[:, None, None] + add_now, state)
    _, prior = lax.scan(carry_state, jnp.zeros_like(local[0]), (whole_decay, local))
    outer = jnp.einsum('bln,bhpn,bhl->blhp', out_blk, prior, jnp.exp(running), precision=highest)
    return (inner + outer).reshape(length, H, P_SIZE)

def mixer(project, dt_raw, conv_weight, conv_bias, dt_bias, a_log, d_skip, gate_gain):
    length = project.shape[0]
    gate_part = project[:, :E]
    conv_in = project[:, E:]
    padded = jnp.pad(conv_in, ((CONVK - 1, 0), (0, 0)))
    conv_out = conv_bias + padded[0:length] * conv_weight[0]
    for offset in range(1, CONVK):
        conv_out = conv_out + padded[offset:offset + length] * conv_weight[offset]
    activ = jax.nn.silu(conv_out)
    values = activ[:, :E].reshape(length, H, P_SIZE)
    in_state = activ[:, E:E + NST]
    out_state = activ[:, E + NST:]
    step_size = jax.nn.softplus(dt_raw + dt_bias)
    log_decay = -jnp.exp(a_log) * step_size
    mixed = ssd_scan(values, step_size, log_decay, in_state, out_state) + d_skip[:, None] * values
    gated = mixed.reshape(length, E) * jax.nn.silu(gate_part)
    return rms_norm(gated, gate_gain)

def reference(tokens, w_in, w_dt, w_out, norm_gain, conv_weight, conv_bias, dt_bias, a_log, d_skip, gate_gain, cotangent):
    count_seqs = tokens.shape[0] // SEQ
    tok_seqs = tokens.reshape(count_seqs, SEQ, D)
    cot_seqs = cotangent.reshape(count_seqs, SEQ, D)
    start_grads = (jnp.zeros(w_in.shape, jnp.float32), jnp.zeros(w_dt.shape, jnp.float32), jnp.zeros(w_out.shape, jnp.float32), jnp.zeros(norm_gain.shape, jnp.float32), jnp.zeros(conv_weight.shape, jnp.float32), jnp.zeros(conv_bias.shape, jnp.float32), jnp.zeros(dt_bias.shape, jnp.float32), jnp.zeros(a_log.shape, jnp.float32), jnp.zeros(d_skip.shape, jnp.float32), jnp.zeros(gate_gain.shape, jnp.float32))

    def one_sequence(grads, item):
        tok, cot = item
        tokens_f = tok.astype(jnp.float32)
        normed_f, norm_pull = jax.vjp(rms_norm, tokens_f, norm_gain)
        normed = normed_f.astype(jnp.bfloat16)
        project = jnp.dot(normed, w_in, preferred_element_type=jnp.float32)
        dt_raw = jnp.dot(normed, w_dt, preferred_element_type=jnp.float32)
        gated_f, mixer_pull = jax.vjp(mixer, project, dt_raw, conv_weight, conv_bias, dt_bias, a_log, d_skip, gate_gain)
        gated = gated_f.astype(jnp.bfloat16)
        result = (tokens_f + jnp.dot(gated, w_out, preferred_element_type=jnp.float32)).astype(jnp.bfloat16)
        grad_out = contract_rows(gated, cot)
        back_gated = contract_cols(cot, w_out)
        pulled = mixer_pull(back_gated)
        back_proj = pulled[0].astype(jnp.bfloat16)
        back_dt = pulled[1].astype(jnp.bfloat16)
        grad_in = contract_rows(normed, back_proj)
        grad_dt = contract_rows(normed, back_dt)
        back_normed = contract_cols(back_proj, w_in) + contract_cols(back_dt, w_dt)
        back_tokens, grad_norm = norm_pull(back_normed)
        token_grad = cot.astype(jnp.float32) + back_tokens
        terms = (grad_in, grad_dt, grad_out, grad_norm) + tuple(pulled[2:])
        new_grads = tuple((total + term for total, term in zip(grads, terms)))
        return (new_grads, (result, token_grad))
    grads, (results, token_grads) = lax.scan(one_sequence, start_grads, (tok_seqs, cot_seqs))
    return (results.reshape(tokens.shape[0], D), token_grads.reshape(tokens.shape[0], D), grads[0], grads[1], grads[2], grads[3], grads[4], grads[5], grads[6], grads[7], grads[8], grads[9])
```

```python
import functools
import jax
import jax.numpy as jnp
import numpy as np
from jax import lax
from jax.experimental import pallas as pl
from jax.experimental.pallas import tpu as pltpu
from jax.sharding import Mesh
from jax.sharding import PartitionSpec as P

H = 80
P_SIZE = 64
E = 5120
NST = 128
CONVK = 4
EPS = 1e-05
Q = 128
CB = 512
HB = CB // P_SIZE
LOG2E = 1.4426950408889634
F32 = jnp.float32
BF16 = jnp.bfloat16
NT = (((1,), (1,)), ((), ()))
TN = (((0,), (0,)), ((), ()))
NN = (((1,), (0,)), ((), ()))


def mm(a, b, dims=NN):
    return lax.dot_general(a, b, dims, preferred_element_type=F32)


def mm_exact(a, b, dims=NN):
    return lax.dot_general(a, b, dims, precision=lax.Precision.HIGHEST, preferred_element_type=F32)


def shifted(before, now):
    stacked = jnp.concatenate([before, now], axis=0)
    return [pltpu.roll(stacked, k, 0)[8:] for k in (1, 2, 3)]


def rows_before(ref, start, lanes):
    prev = ref[pl.ds(pl.multiple_of(jnp.maximum(start - 8, 0), 8), 8), lanes]
    return jnp.where(start > 0, prev, 0.0)


def conv_of(now, past, taps, bias):
    return (
        bias
        + past[2] * taps[0:1]
        + past[1] * taps[1:2]
        + past[0] * taps[2:3]
        + now * taps[3:4]
    )


def fold8(x):
    total = x[0:8]
    for k in range(1, x.shape[0] // 8):
        total = total + x[8 * k : 8 * k + 8]
    return total


def lower_tri():
    return lax.broadcasted_iota(jnp.int32, (Q, Q), 0) >= lax.broadcasted_iota(jnp.int32, (Q, Q), 1)


def prepare_kernel(ps_ref, cw_ref, cb_ref, dtb_ref, al_ref, b_ref, c_ref, bt_ref, ct_ref, g_ref, run_ref, step_ref):
    tri = lower_tri()
    ones = tri.astype(F32)

    def chunk(c, carry):
        start = pl.multiple_of(c * Q, Q)
        rows = pl.ds(start, Q)
        state = []
        for j in range(2):
            lanes = slice(NST * j, NST * (j + 1))
            now = ps_ref[rows, lanes]
            past = shifted(rows_before(ps_ref, start, lanes), now)
            co = conv_of(now, past, cw_ref[:, lanes], cb_ref[:, lanes])
            state.append(co * jax.nn.sigmoid(co))
        ins, outs = state
        b_ref[rows, :] = ins.astype(BF16)
        c_ref[rows, :] = outs.astype(BF16)
        bt_ref[:, rows] = ins.T.astype(BF16)
        ct_ref[:, rows] = outs.T.astype(BF16)
        g_ref[rows, :] = jnp.where(tri, mm_exact(outs, ins, NT), 0.0)
        step = jax.nn.softplus(ps_ref[rows, 2 * NST : 3 * NST] + dtb_ref[...])
        decay = -jnp.exp(al_ref[...]) * step
        run = mm_exact(ones, decay) * LOG2E
        run_ref[:, rows] = run.T
        step_ref[:, rows] = step.T
        return carry

    lax.fori_loop(0, ps_ref.shape[0] // Q, chunk, 0)


def prepare(ps, cw, cb, dtb, al):
    tokens = ps.shape[0]
    return pl.pallas_call(
        prepare_kernel,
        out_shape=(
            jax.ShapeDtypeStruct((tokens, NST), BF16),
            jax.ShapeDtypeStruct((tokens, NST), BF16),
            jax.ShapeDtypeStruct((NST, tokens), BF16),
            jax.ShapeDtypeStruct((NST, tokens), BF16),
            jax.ShapeDtypeStruct((tokens, Q), F32),
            jax.ShapeDtypeStruct((128, tokens), F32),
            jax.ShapeDtypeStruct((128, tokens), F32),
        ),
        compiler_params=pltpu.CompilerParams(vmem_limit_bytes=40 << 20),
        cost_estimate=pl.CostEstimate(flops=600000000, bytes_accessed=int(5e6), transcendentals=1000000),
        name="prepare",
    )(ps, cw, cb, dtb, al)


def pair_select(first, cols, j):
    return jnp.where(first, cols[:, 2 * j : 2 * j + 1], cols[:, 2 * j + 1 : 2 * j + 2])


def forward_kernel(
    both_ref, bg_ref, run_ref, step_ref, c_ref, bt_ref, g_ref, cw_ref, cb_ref, dsk_ref, gain_ref,
    mixed_ref, y_ref, prior_ref, ss_ref, cg_ref, state,
):
    first = lax.broadcasted_iota(jnp.int32, (1, 128), 1) < P_SIZE
    state[...] = jnp.zeros_like(state)

    @pl.when(pl.program_id(0) == 0)
    def _():
        ss_ref[...] = jnp.zeros_like(ss_ref)
        cg_ref[...] = jnp.zeros_like(cg_ref)

    def chunk(c, carry):
        start = pl.multiple_of(c * Q, Q)
        rows = pl.ds(start, Q)
        run_rows = run_ref[:, rows]
        run_cols = run_rows.T
        step_cols = step_ref[:, rows].T
        run_end = run_cols[Q - 1 : Q, :]
        outs = c_ref[rows, :]
        ins_t = bt_ref[:, rows]
        meet = g_ref[rows, :]
        squares = jnp.zeros((Q, 128), F32)
        products = jnp.zeros((Q, 128), F32)
        for j in range(CB // 128):
            lanes = slice(128 * j, 128 * (j + 1))
            below = slice(CB + 128 * j, CB + 128 * (j + 1))
            now = both_ref[rows, below].astype(F32)
            past = shifted(rows_before(both_ref, start, below).astype(F32), now)
            co = conv_of(now, past, cw_ref[:, lanes], cb_ref[:, lanes])
            values = co * jax.nn.sigmoid(co)
            run_pair = pair_select(first, run_cols, j)
            end_pair = pair_select(first, run_end, j)
            weighted = pair_select(first, step_cols, j) * values
            stacked = jnp.concatenate(
                [jnp.where(first, weighted, 0.0), jnp.where(first, 0.0, weighted)], axis=0
            ).astype(BF16)
            scores = []
            for h in (2 * j, 2 * j + 1):
                gap = run_cols[:, h : h + 1] - run_rows[h : h + 1, :]
                scores.append((jnp.exp2(jnp.minimum(gap, 0.0)) * meet).astype(BF16))
            inner = mm(jnp.concatenate(scores, axis=1), stacked)
            held = state[:, lanes]
            held_b = held.astype(BF16)
            outer = mm(outs, held_b) * jnp.exp2(run_pair)
            mixed = inner + outer + dsk_ref[:, lanes] * values
            gate = both_ref[rows, lanes].astype(F32)
            y = mixed * (gate * jax.nn.sigmoid(gate))
            mixed_ref[rows, lanes] = mixed.astype(BF16)
            y_ref[rows, lanes] = y.astype(BF16)
            squares = squares + y * y
            products = products + bg_ref[rows, lanes].astype(F32) * gain_ref[:, lanes] * y
            prior_ref[rows, lanes] = held_b
            add = mm(ins_t, (jnp.exp2(end_pair - run_pair) * weighted).astype(BF16))
            state[:, lanes] = held * jnp.exp2(end_pair) + add
        ss_ref[rows, :] += squares
        cg_ref[rows, :] += products
        return carry

    lax.fori_loop(0, both_ref.shape[0] // Q, chunk, 0)


def forward(proj, bg, col0, prep, cw, cb, dsk, gain):
    tokens, width = proj.shape[0], proj.shape[1] // 2
    steps = width // CB
    first = col0 // CB
    ins, outs, ins_t, outs_t, meet, run, step = prep

    def whole(shape):
        return pl.BlockSpec(shape, lambda i: (0, 0))

    def cols(rows, base, wide=CB):
        return pl.BlockSpec((rows, wide), lambda i: (0, i + base))

    def heads():
        return pl.BlockSpec((HB, tokens), lambda i: (i + first, 0))

    return pl.pallas_call(
        forward_kernel,
        grid=(steps,),
        in_specs=[
            cols(tokens, 0, 2 * CB), cols(tokens, first), heads(), heads(),
            whole((tokens, NST)), whole((NST, tokens)), whole((tokens, Q)),
            cols(CONVK, first), cols(1, first), cols(1, first), cols(1, first),
        ],
        out_specs=[
            cols(tokens, 0), cols(tokens, 0), cols(tokens, 0), whole((tokens, 128)), whole((tokens, 128)),
        ],
        out_shape=(
            jax.ShapeDtypeStruct((tokens, width), BF16),
            jax.ShapeDtypeStruct((tokens, width), BF16),
            jax.ShapeDtypeStruct((tokens, width), BF16),
            jax.ShapeDtypeStruct((tokens, 128), F32),
            jax.ShapeDtypeStruct((tokens, 128), F32),
        ),
        scratch_shapes=[pltpu.VMEM((NST, CB), F32)],
        compiler_params=pltpu.CompilerParams(vmem_limit_bytes=48 << 20),
        cost_estimate=pl.CostEstimate(
            flops=int(tokens * width * 4000), bytes_accessed=int(tokens * width * 18), transcendentals=int(tokens * width * 5)
        ),
        name="forward",
    )(proj, bg, run, step, outs, ins_t, meet, cw, cb, dsk, gain)


def backward_kernel(
    head0,
    both_ref, bg_ref, mixed_ref, prior_ref, run_ref, step_ref, b_ref, c_ref, ct_ref, g_ref, r_ref, k_ref,
    cw_ref, cb_ref, dsk_ref, gain_ref,
    dboth_ref, f_ref, ds_ref, dg_ref, dc_ref, db_ref, vec_ref, dstate, ahead,
):
    first = lax.broadcasted_iota(jnp.int32, (1, 128), 1) < P_SIZE
    last_row = lax.broadcasted_iota(jnp.int32, (Q, 1), 0) == Q - 1
    dstate[...] = jnp.zeros_like(dstate)
    ahead[...] = jnp.zeros_like(ahead)
    vec_ref[...] = jnp.zeros_like(vec_ref)

    @pl.when(pl.program_id(0) == 0)
    def _():
        for ref in (f_ref, ds_ref, dg_ref, dc_ref, db_ref):
            ref[...] = jnp.zeros_like(ref)

    head = lax.broadcasted_iota(jnp.int32, (CB, 128), 0) // P_SIZE + (head0 + HB * pl.program_id(0))
    pick = (head == lax.broadcasted_iota(jnp.int32, (CB, 128), 1)).astype(BF16)
    count = both_ref.shape[0] // Q

    def chunk(i, carry):
        c = count - 1 - i
        start = pl.multiple_of(c * Q, Q)
        rows = pl.ds(start, Q)
        run_rows = run_ref[:, rows]
        run_cols = run_rows.T
        step_cols = step_ref[:, rows].T
        run_end = run_cols[Q - 1 : Q, :]
        outs = c_ref[rows, :]
        ins = b_ref[rows, :]
        outs_t = ct_ref[:, rows]
        meet = g_ref[rows, :]
        scale = r_ref[rows, :]
        pull = k_ref[rows, :]
        dmeet = jnp.zeros((Q, Q), F32)
        douts = jnp.zeros((Q, NST), F32)
        dins = jnp.zeros((Q, NST), F32)
        runs_hi, runs_lo, steps_hi, steps_lo = [], [], [], []
        for j in range(CB // 128):
            lanes = slice(128 * j, 128 * (j + 1))
            below = slice(CB + 128 * j, CB + 128 * (j + 1))
            now = both_ref[rows, below].astype(F32)
            past = shifted(rows_before(both_ref, start, below).astype(F32), now)
            taps = cw_ref[:, lanes]
            co = conv_of(now, past, taps, cb_ref[:, lanes])
            co_sig = jax.nn.sigmoid(co)
            values = co * co_sig
            gate = both_ref[rows, lanes].astype(F32)
            gate_sig = jax.nn.sigmoid(gate)
            gate_silu = gate * gate_sig
            mixed = mixed_ref[rows, lanes].astype(F32)
            y = mixed * gate_silu
            scaled = bg_ref[rows, lanes].astype(F32) * scale
            vec_ref[40:48, lanes] += fold8(scaled * y)
            dy = scaled * gain_ref[:, lanes] - y * pull
            dmix = dy * gate_silu
            dgate = dy * mixed * (gate_sig + gate_silu * (1.0 - gate_sig))
            dboth_ref[rows, lanes] = dgate.astype(BF16)
            vec_ref[48:56, lanes] += fold8(dmix * values)

            run_pair = pair_select(first, run_cols, j)
            end_pair = pair_select(first, run_end, j)
            step_pair = pair_select(first, step_cols, j)
            weighted = step_pair * values
            stacked = jnp.concatenate(
                [jnp.where(first, weighted, 0.0), jnp.where(first, 0.0, weighted)], axis=0
            ).astype(BF16)
            rounded = weighted.astype(BF16).astype(F32)
            dmix_b = dmix.astype(BF16)
            fade_in = jnp.exp2(run_pair)
            fade_out = jnp.exp2(end_pair - run_pair)
            dmix_in = (fade_in * dmix).astype(BF16)
            kept = (fade_out * weighted).astype(BF16)
            prior = prior_ref[rows, lanes]
            dnext = dstate[:, lanes]
            dnext_b = dnext.astype(BF16)
            outer = mm(outs, prior)
            dkept = mm(ins, dnext_b)
            fades, scores = [], []
            for h in (2 * j, 2 * j + 1):
                gap = run_cols[:, h : h + 1] - run_rows[h : h + 1, :]
                fade = jnp.exp2(jnp.minimum(gap, 0.0))
                fades.append(fade)
                scores.append((fade * meet).astype(BF16))
            scores = jnp.concatenate(scores, axis=1)
            inner = mm(scores, stacked)
            both = mm(scores, dmix_b, TN)
            dinner = jnp.where(first, both[:Q], both[Q:])
            dscores = mm(dmix_b, stacked, NT)
            dmeet = dmeet + dscores[:, :Q] * fades[0] + dscores[:, Q:] * fades[1]
            kept_flow = kept.astype(F32) * dkept
            end_decay = jnp.exp2(end_pair)
            at_end = jnp.sum(kept_flow, axis=0, keepdims=True) + end_decay * jnp.sum(
                dnext * prior.astype(F32), axis=0, keepdims=True
            )
            flow = (
                dmix_b.astype(F32) * inner
                + dmix_in.astype(F32) * outer
                - rounded * dinner
                - kept_flow
                + jnp.where(last_row, at_end, 0.0)
            )
            flow_hi = flow.astype(BF16)
            runs_hi.append(flow_hi)
            runs_lo.append((flow - flow_hi.astype(F32)).astype(BF16))
            dweighted = dinner + fade_out * dkept
            dstep = dweighted * values
            dstep_hi = dstep.astype(BF16)
            steps_hi.append(dstep_hi)
            steps_lo.append((dstep - dstep_hi.astype(F32)).astype(BF16))
            dvalues = step_pair * dweighted + dsk_ref[:, lanes] * dmix
            dco = dvalues * (co_sig + values * (1.0 - co_sig))
            for k, source in enumerate((past[2], past[1], past[0], now)):
                vec_ref[8 * k : 8 * k + 8, lanes] += fold8(dco * source)
            vec_ref[32:40, lanes] += fold8(dco)
            spread = jnp.concatenate([dco, ahead[:, lanes]], axis=0)
            ahead[:, lanes] = dco[0:8]
            dconv = dco * taps[3:4]
            for k in (1, 2, 3):
                dconv = dconv + pltpu.roll(spread, Q + 8 - k, 0)[:Q] * taps[3 - k : 4 - k]
            dboth_ref[rows, below] = dconv.astype(BF16)
            douts = douts + mm(dmix_in, prior, NT)
            dins = dins + mm(kept, dnext_b, NT)
            dstate[:, lanes] = dnext * end_decay + mm(outs_t, dmix_in)
        dg_ref[rows, :] += dmeet
        dc_ref[rows, :] += douts
        db_ref[rows, :] += dins
        f_ref[rows, :] += mm(jnp.concatenate(runs_hi, axis=1), pick) + mm(jnp.concatenate(runs_lo, axis=1), pick)
        ds_ref[rows, :] += mm(jnp.concatenate(steps_hi, axis=1), pick) + mm(jnp.concatenate(steps_lo, axis=1), pick)
        return carry

    lax.fori_loop(0, count, chunk, 0)


def backward(proj, bg, mixed, prior, col0, prep, scale, pull, cw, cb, dsk, gain):
    tokens, width = proj.shape[0], proj.shape[1] // 2
    steps = width // CB
    first = col0 // CB
    ins, outs, ins_t, outs_t, meet, run, step = prep

    def whole(shape):
        return pl.BlockSpec(shape, lambda i: (0, 0))

    def cols(rows, base, wide=CB):
        return pl.BlockSpec((rows, wide), lambda i: (0, i + base))

    def heads():
        return pl.BlockSpec((HB, tokens), lambda i: (i + first, 0))

    return pl.pallas_call(
        functools.partial(backward_kernel, col0 // P_SIZE),
        grid=(steps,),
        in_specs=[
            cols(tokens, 0, 2 * CB), cols(tokens, first), cols(tokens, 0), cols(tokens, 0),
            heads(), heads(),
            whole((tokens, NST)), whole((tokens, NST)), whole((NST, tokens)), whole((tokens, Q)),
            whole((tokens, 128)), whole((tokens, 128)),
            cols(CONVK, first), cols(1, first), cols(1, first), cols(1, first),
        ],
        out_specs=[cols(tokens, 0, 2 * CB)] + [whole((tokens, 128))] * 5 + [cols(56, 0)],
        out_shape=(jax.ShapeDtypeStruct((tokens, 2 * width), BF16),)
        + (jax.ShapeDtypeStruct((tokens, 128), F32),) * 5
        + (jax.ShapeDtypeStruct((56, width), F32),),
        scratch_shapes=[pltpu.VMEM((NST, CB), F32), pltpu.VMEM((8, CB), F32)],
        compiler_params=pltpu.CompilerParams(vmem_limit_bytes=56 << 20),
        cost_estimate=pl.CostEstimate(
            flops=int(tokens * width * 12000), bytes_accessed=int(tokens * width * 20), transcendentals=int(tokens * width * 8)
        ),
        name="backward",
    )(proj, bg, mixed, prior, run, step, ins, outs, outs_t, meet, scale, pull, cw, cb, dsk, gain)


def finish_kernel(
    ps_ref, cw_ref, cb_ref, dtb_ref, al_ref, f_ref, ds_ref, dg_ref, dc_ref, db_ref,
    out_ref, vec_ref, ahead,
):
    tri = lower_tri()
    later = (
        lax.broadcasted_iota(jnp.int32, (Q, Q), 0) <= lax.broadcasted_iota(jnp.int32, (Q, Q), 1)
    ).astype(F32)
    vec_ref[...] = jnp.zeros_like(vec_ref)
    ahead[...] = jnp.zeros_like(ahead)
    count = ps_ref.shape[0] // Q

    def chunk(i, carry):
        c = count - 1 - i
        start = pl.multiple_of(c * Q, Q)
        rows = pl.ds(start, Q)
        convs, sigs, pasts, nows = [], [], [], []
        for j in range(2):
            lanes = slice(NST * j, NST * (j + 1))
            now = ps_ref[rows, lanes]
            past = shifted(rows_before(ps_ref, start, lanes), now)
            co = conv_of(now, past, cw_ref[:, lanes], cb_ref[:, lanes])
            convs.append(co)
            sigs.append(jax.nn.sigmoid(co))
            pasts.append(past)
            nows.append(now)
        ins, outs = convs[0] * sigs[0], convs[1] * sigs[1]
        dmeet = jnp.where(tri, dg_ref[rows, :], 0.0)
        dins = mm_exact(dmeet, outs, TN) + db_ref[rows, :]
        douts = mm_exact(dmeet, ins) + dc_ref[rows, :]
        for j, (grad, act) in enumerate(((dins, ins), (douts, outs))):
            lanes = slice(NST * j, NST * (j + 1))
            dco = grad * (sigs[j] + act * (1.0 - sigs[j]))
            for k, source in enumerate((pasts[j][2], pasts[j][1], pasts[j][0], nows[j])):
                vec_ref[8 * k : 8 * k + 8, lanes] += fold8(dco * source)
            vec_ref[32:40, lanes] += fold8(dco)
            spread = jnp.concatenate([dco, ahead[:, lanes]], axis=0)
            ahead[:, lanes] = dco[0:8]
            taps = cw_ref[:, lanes]
            dconv = dco * taps[3:4]
            for k in (1, 2, 3):
                dconv = dconv + pltpu.roll(spread, Q + 8 - k, 0)[:Q] * taps[3 - k : 4 - k]
            out_ref[rows, lanes] = dconv.astype(BF16)
        dt = slice(2 * NST, 3 * NST)
        before = ps_ref[rows, dt] + dtb_ref[...]
        rate = -jnp.exp(al_ref[...])
        ddecay = mm_exact(later, f_ref[rows, :])
        ddt = (ds_ref[rows, :] + rate * ddecay) * jax.nn.sigmoid(before)
        vec_ref[0:8, dt] += fold8(ddt)
        vec_ref[8:16, dt] += fold8(ddecay * rate * jax.nn.softplus(before))
        out_ref[rows, dt] = ddt.astype(BF16)
        return carry

    lax.fori_loop(0, count, chunk, 0)


def finish(ps, cw, cb, dtb, al, f, ds, dg, dc, db):
    tokens = ps.shape[0]
    return pl.pallas_call(
        finish_kernel,
        out_shape=(jax.ShapeDtypeStruct((tokens, 384), BF16), jax.ShapeDtypeStruct((40, 384), F32)),
        scratch_shapes=[pltpu.VMEM((8, 256), F32)],
        compiler_params=pltpu.CompilerParams(vmem_limit_bytes=40 << 20),
        cost_estimate=pl.CostEstimate(flops=800000000, bytes_accessed=int(6e6), transcendentals=1000000),
        name="finish",
    )(ps, cw, cb, dtb, al, f, ds, dg, dc, db)


CHUNKS = ((0, 2), (2, 2), (4, 2), (6, 2), (8, 2))


def rms_norm(tokens_f, gain):
    return tokens_f * lax.rsqrt(jnp.mean(tokens_f * tokens_f, axis=-1, keepdims=True) + EPS) * gain


def chunk_columns(weight, first, steps):
    parts = []
    for s in range(first, first + steps):
        parts.append(weight[:, CB * s : CB * (s + 1)])
        parts.append(weight[:, E + CB * s : E + CB * (s + 1)])
    return jnp.concatenate(parts, axis=1)


def half_rows(weight):
    rows = weight.shape[0] // 2
    return lax.dynamic_slice_in_dim(weight, lax.axis_index("core") * rows, rows, 0)


def gather(half):
    return lax.all_gather(half, ("shard", "core"), axis=0, tiled=True)


def reduce_rows(grad):
    part = lax.psum_scatter(grad, ("shard", "core"), scatter_dimension=0, tiled=True)
    part = lax.psum(part, "far")
    return lax.all_gather(part, "core", axis=0, tiled=True)


def butterfly(value):
    for name in ("core", "shard", "far"):
        size = lax.axis_size(name)
        hop = 1
        while hop < size:
            value = value + lax.ppermute(value, name, [(i, i ^ hop) for i in range(size)])
            hop *= 2
    return value


def body(tokens, w_in, w_dt, w_out, norm_gain, conv_weight, conv_bias, dt_bias, a_log, d_skip, gate_gain, cotangent):
    length = tokens.shape[0]
    tokens_f = tokens.astype(F32)
    half_in = half_rows(w_in)
    side = jnp.concatenate(
        [half_in[:, 2 * E :], half_rows(w_dt), jnp.zeros((half_in.shape[0], 128 - H), BF16)], axis=1
    )
    w_side = gather(side)
    w_out_full = gather(half_rows(w_out))
    w_chunks = [gather(chunk_columns(half_in, first, steps)) for first, steps in CHUNKS]

    normed_f, norm_pull = jax.vjp(rms_norm, tokens_f, norm_gain)
    normed = normed_f.astype(BF16)
    bg = mm(cotangent, w_out_full, NT)

    cw, cb = conv_weight, conv_bias[None]
    cws, cbs = cw[:, E:], cb[:, E:]
    dtb = jnp.pad(dt_bias, (0, 128 - H))[None]
    al = jnp.pad(a_log, (0, 128 - H))[None]
    dsk = jnp.repeat(d_skip, P_SIZE)[None]
    gain = gate_gain[None]

    ps = mm(normed, w_side)
    prep = prepare(ps, cws, cbs, dtb, al)
    projs, fronts = [], []
    for (first, steps), weight in zip(CHUNKS, w_chunks):
        projs.append(mm(normed, weight))
        fronts.append(forward(projs[-1], bg, CB * first, prep, cw, cb, dsk, gain))
    ss = sum(f[3] for f in fronts).sum(axis=1, keepdims=True)
    cg = sum(f[4] for f in fronts).sum(axis=1, keepdims=True)
    r = lax.rsqrt(ss / E + EPS)
    k = r * r * r * cg / E
    scale = jnp.broadcast_to(r, (length, 128))
    pull = jnp.broadcast_to(k, (length, 128))
    y = jnp.concatenate([f[1] for f in fronts], axis=1)
    gated = (y.astype(F32) * r * gain).astype(BF16)
    grad_out = reduce_rows(mm(gated, cotangent, TN).astype(BF16)).astype(F32)
    result = (tokens_f + mm(gated, w_out_full)).astype(BF16)

    totals, vecs, parts = None, [], []
    back = None
    for (first, steps), weight, proj, front in zip(CHUNKS, w_chunks, projs, fronts):
        dproj, *sums, vec = backward(
            proj, bg, front[0], front[2], CB * first, prep, scale, pull, cw, cb, dsk, gain
        )
        totals = sums if totals is None else [a + b for a, b in zip(totals, sums)]
        vecs.append(vec)
        parts.append(reduce_rows(mm(normed, dproj, TN).astype(BF16)))
        term = mm(dproj, weight, NT)
        back = term if back is None else back + term
    dside, svec = finish(ps, cws, cbs, dtb, al, *totals)
    part_side = reduce_rows(mm(normed, dside, TN).astype(BF16))
    back = back + mm(dside, w_side, NT)

    gates, convs = [], []
    for (first, steps), part in zip(CHUNKS, parts):
        for s in range(steps):
            gates.append(part[:, 2 * CB * s : 2 * CB * s + CB])
            convs.append(part[:, 2 * CB * s + CB : 2 * CB * (s + 1)])
    grad_in = jnp.concatenate(gates + convs + [part_side[:, : 2 * NST]], axis=1).astype(F32)
    grad_dt = part_side[:, 2 * NST : 2 * NST + H].astype(F32)

    back_tokens, grad_norm = norm_pull(back)
    token_grad = cotangent.astype(F32) + back_tokens

    vec = jnp.concatenate([v.reshape(7, 8, -1).sum(axis=1) for v in vecs], axis=1)
    svec = svec.reshape(5, 8, -1).sum(axis=1)
    pieces = [
        grad_norm,
        jnp.concatenate([vec[:CONVK], svec[:CONVK, : 2 * NST]], axis=1).reshape(-1),
        jnp.concatenate([vec[CONVK], svec[CONVK, : 2 * NST]]),
        svec[0, 2 * NST : 2 * NST + H],
        svec[1, 2 * NST : 2 * NST + H],
        vec[6].reshape(H, P_SIZE).sum(axis=1),
        vec[5],
    ]
    packed = jnp.concatenate(pieces)
    packed = jnp.pad(packed, (0, -packed.size % 1024)).reshape(-1, 128)
    packed = butterfly(packed).reshape(-1)
    smalls, at = [], 0
    for piece in pieces:
        smalls.append(packed[at : at + piece.size])
        at += piece.size
    return (
        result, token_grad, grad_in, grad_dt, grad_out,
        smalls[0], smalls[1].reshape(CONVK, -1), *smalls[2:],
    )


def solution(mesh):
    replicas, shards = mesh.shape["replica"], mesh.shape["shard"]
    cores = 2 if replicas % 2 == 0 else 1
    inner = Mesh(mesh.devices.reshape(replicas // cores, cores, shards), ("far", "core", "shard"))
    rows = P(("far", "core", "shard"), None)
    held = P("shard", None)
    return jax.shard_map(
        body,
        mesh=inner,
        in_specs=(rows, held, held, held) + (P(),) * 7 + (rows,),
        out_specs=(rows, rows, held, held, held) + (P(),) * 7,
        check_vma=False,
    )
```
